32 devices in a mesh: dp: 4 (over y, core), fsdp: 8 (over z, x).
Axes of the slice: x: 2, y: 2, z: 4, core: 2. Of those that a mesh axis runs over, the one named last changes fastest.
Arguments:
- tokens: bfloat16 [32768, 576], P(('dp', 'fsdp')), may hold values from -6 to 6
- segments: int32 [32, 1024], P(('dp', 'fsdp')), may hold values from 0 to 2, as said below
- positions: int32 [32, 1024], P(('dp', 'fsdp')), may hold values from 0 to 2302, as said below
- attn_gain: bfloat16 [576], P('fsdp'), may hold values from 0.25 to 1.75
- mlp_gain: bfloat16 [576], P('fsdp'), may hold values from 0.25 to 1.75
- w_query: bfloat16 [576, 576], P('fsdp', 'dp'), may hold values from -0.375 to 0.375
- w_key: bfloat16 [576, 192], P('fsdp', 'dp'), may hold values from -0.375 to 0.375
- w_value: bfloat16 [576, 192], P('fsdp', 'dp'), may hold values from -0.25 to 0.25
- w_output: bfloat16 [576, 576], P('dp', 'fsdp'), may hold values from -1 to 1
- w_gate: bfloat16 [576, 1536], P('fsdp', 'dp'), may hold values from -0.25 to 0.25
- w_up: bfloat16 [576, 1536], P('fsdp', 'dp'), may hold values from -0.25 to 0.25
- w_down: bfloat16 [1536, 576], P('dp', 'fsdp'), may hold values from -0.21875 to 0.21875
- cotangent: bfloat16 [32768, 576], P(('dp', 'fsdp')), may hold values from -6 to 6
Outputs:
- output: bfloat16 [32768, 576], P(('dp', 'fsdp'))
- grad_tokens: float32 [32768, 576], P(('dp', 'fsdp'))
- grad_attn_gain: float32 [576], P('fsdp')
- grad_mlp_gain: float32 [576], P('fsdp')
- grad_query: float32 [576, 576], P('fsdp', 'dp')
- grad_key: float32 [576, 192], P('fsdp', 'dp')
- grad_value: float32 [576, 192], P('fsdp', 'dp')
- grad_output: float32 [576, 576], P('dp', 'fsdp')
- grad_gate: float32 [576, 1536], P('fsdp', 'dp')
- grad_up: float32 [576, 1536], P('fsdp', 'dp')
- grad_down: float32 [1536, 576], P('dp', 'fsdp')
The draws below stay inside these ranges and needn't reach their ends.
Inputs may be any that keep to these rules, and one draw needn't show every extreme that they name: `segments`: in each sequence the document numbers are 0, then 1, then 2, each a run of 128 tokens or more. `positions`: counts up by one along a document; documents 1 and 2 of a sequence begin at 0, document 0 continues a document begun at most 2047 tokens before the sequence and ends within its first 256 tokens.
All inputs are finite; a program needn't handle non-finite values.
Results may differ from the reference program's by a relative error of at most 0.015.
The reference program's roundings to bfloat16 on the way count: a program that leaves them out, or rounds other values in their place, can miss the bound.
Values may be sent and summed in bfloat16 or wider, within the bound.
A program may use at most 192 MiB of HBM per device.

```python
import jax
import jax.numpy as jnp
from jax import lax

D = 576
Q_HEADS = 9
KV_HEADS = 3
HEAD_DIM = 64
FF = 1536
LEN = 1024
QBLOCK = 512
QW = 576
KVW = 192
SEQS = 32
TOKENS = 32768


def packing(key):
    base = jax.random.fold_in(key, 7)
    first_key, second_key, offset_key = jax.random.split(base, 3)
    first = jax.random.randint(first_key, (SEQS, 1), LEN // 8, LEN // 4 + 1)
    first = first.at[0, 0].set(LEN // 4)
    second = first + jax.random.randint(second_key, (SEQS, 1), LEN // 5, LEN // 2 + 1)
    offset = jax.random.randint(offset_key, (SEQS, 1), 0, 2 * LEN)
    offset = offset.at[0, 0].set(2 * LEN - 1)
    index = jnp.arange(LEN, dtype=jnp.int32)[None, :]
    segment = (index >= first).astype(jnp.int32) + (index >= second).astype(jnp.int32)
    begin = jnp.where(index >= second, second, jnp.where(index >= first, first, -offset))
    return (segment, (index - begin).astype(jnp.int32))


def draw_segments(key, part):
    return packing(key)[0]


def draw_positions(key, part):
    return packing(key)[1]


def block_scale(stream_key, shape, pieces, least, largest):
    factor_of, own = 1.0, jax.random.fold_in(stream_key, 6)
    for axis_at, parts in pieces:
        draws = jnp.exp(jax.random.uniform(jax.random.fold_in(own, axis_at), (parts,), jnp.float32, least / len(pieces), largest / len(pieces)))
        factor_of = factor_of * jnp.repeat(draws, shape[axis_at] // parts).reshape([-1 if axis == axis_at else 1 for axis in range(len(shape))])
    return factor_of


def normal_values(stream_key, extent, scale, limit, cuts=(), kind=jnp.bfloat16):
    drawn = scale * jax.random.normal(stream_key, extent, jnp.float32)
    if cuts:
        drawn = drawn * block_scale(stream_key, extent, cuts, -0.22, 0.18)
    return jnp.clip(drawn, -limit, limit).astype(kind)


def setup_inputs(seed: int = 0) -> dict:
    key_list = jax.random.split(jax.random.key(seed), 14)
    tokens = normal_values(key_list[0], (TOKENS, D), 1.0, 6.0, ((0, 32),))
    segments = draw_segments(jax.random.fold_in(key_list[13], 71), 0)
    positions = draw_positions(jax.random.fold_in(key_list[13], 71), 0)
    attn_gain = jnp.clip(1.0 + 0.15 * jax.random.normal(key_list[3], (D,), jnp.float32), 0.25, 1.75).astype(jnp.bfloat16)
    mlp_gain = jnp.clip(1.0 + 0.15 * jax.random.normal(key_list[4], (D,), jnp.float32), 0.25, 1.75).astype(jnp.bfloat16)
    w_query = normal_values(key_list[5], (D, QW), (D // 2) ** -0.5, 0.375, ((0, 8), (1, 4)))
    w_key = normal_values(key_list[6], (D, KVW), (D // 2) ** -0.5, 0.375, ((0, 8), (1, 4)))
    w_value = normal_values(key_list[7], (D, KVW), D ** -0.5, 0.25, ((0, 8), (1, 4)))
    w_output = normal_values(key_list[8], (QW, D), (max(QW // 16, 1)) ** -0.5, 1.0, ((0, 4), (1, 8)))
    w_gate = normal_values(key_list[9], (D, FF), D ** -0.5, 0.25, ((0, 8), (1, 4)))
    w_up = normal_values(key_list[10], (D, FF), D ** -0.5, 0.25, ((0, 8), (1, 4)))
    w_down = normal_values(key_list[11], (FF, D), (FF // 2) ** -0.5, 0.21875, ((0, 4), (1, 8)))
    cotangent = normal_values(key_list[12], (TOKENS, D), 1.0, 6.0, ((0, 32),))
    return {"tokens": tokens, "segments": segments, "positions": positions, "attn_gain": attn_gain, "mlp_gain": mlp_gain, "w_query": w_query, "w_key": w_key, "w_value": w_value, "w_output": w_output, "w_gate": w_gate, "w_up": w_up, "w_down": w_down, "cotangent": cotangent}


EPS = 1e-05
ROPE_BASE = 100000.0
MASKED = -1e+30
HIGH = lax.Precision.HIGHEST

@jax.custom_vjp
def low(v):
    return lax.optimization_barrier(v.astype(jnp.bfloat16)).astype(jnp.float32)

@jax.custom_vjp
def low_back(v):
    return v

def low_keep(v):
    return (low(v), None)

def low_pass(kept, grad):
    return (grad,)

def back_keep(v):
    return (v, None)

def back_low(kept, grad):
    return (low(grad),)
low.defvjp(low_keep, low_pass)
low_back.defvjp(back_keep, back_low)

def matmul(left, right):
    return jnp.dot(left, right, preferred_element_type=jnp.float32, precision=HIGH)

def tables(position):
    half_dim = HEAD_DIM // 2
    frequency = ROPE_BASE ** (-(2.0 * jnp.arange(half_dim, dtype=jnp.float32)) / HEAD_DIM)
    angles = position.astype(jnp.float32)[:, None] * frequency[None, :]
    angles = jnp.concatenate([angles, angles], axis=1)
    return (jnp.cos(angles), jnp.sin(angles))

def rotate(values, cosine, sine_table):
    half_dim = HEAD_DIM // 2
    turned = jnp.concatenate([-values[..., half_dim:], values[..., :half_dim]], axis=-1)
    return values * cosine[:, None, :] + turned * sine_table[:, None, :]

def norm_rows(values, gain):
    inverse = lax.rsqrt(lax.optimization_barrier(jnp.mean(values * values, axis=-1, keepdims=True)) + EPS)
    return values * inverse * gain

def attend(queries, keys, values, segment):
    group_size = Q_HEADS // KV_HEADS
    blocks = LEN // QBLOCK
    grouped = queries.reshape(blocks, QBLOCK, KV_HEADS, group_size, HEAD_DIM)
    block_segments = segment.reshape(blocks, QBLOCK)
    starts = jnp.arange(blocks, dtype=jnp.int32) * QBLOCK
    scale = HEAD_DIM ** (-0.5)
    col_index = jnp.arange(LEN, dtype=jnp.int32)

    def one_block(block_data):
        query_block, seg_block, block_start = block_data
        row_index = block_start + jnp.arange(QBLOCK, dtype=jnp.int32)
        allowed = (col_index[None, :] <= row_index[:, None]) & (segment[None, :] == seg_block[:, None])
        scores = low_back(jnp.einsum('qkgd,tkd->kgqt', query_block, keys, precision=HIGH) * scale)
        scores = jnp.where(allowed[None, None], scores, MASKED)
        top_value = lax.optimization_barrier(jnp.max(scores, axis=-1, keepdims=True))
        expo = jnp.exp(scores - top_value)
        probability = low(expo / lax.optimization_barrier(jnp.sum(expo, axis=-1, keepdims=True)))
        return jnp.einsum('kgqt,tkd->qkgd', probability, values, precision=HIGH)
    attended = lax.map(jax.checkpoint(one_block), (grouped, block_segments, starts))
    return attended.reshape(LEN, QW)

def layer(rows, segment, position, params):
    gain_attn, gain_mlp, w_query, w_key, w_value, w_output, w_gate, w_up, w_down = params
    cosine, sine_table = tables(position)
    normed_attn = low(norm_rows(rows, gain_attn))
    query_raw = low_back(matmul(normed_attn, w_query))
    key_raw = low_back(matmul(normed_attn, w_key))
    value_raw = low_back(matmul(normed_attn, w_value))
    queries = low(rotate(query_raw.reshape(LEN, Q_HEADS, HEAD_DIM), cosine, sine_table))
    keys = low(rotate(key_raw.reshape(LEN, KV_HEADS, HEAD_DIM), cosine, sine_table))
    values = low(value_raw).reshape(LEN, KV_HEADS, HEAD_DIM)
    mixture = low(low_back(attend(queries, keys, values, segment)))
    resid = rows + low_back(matmul(mixture, w_output))
    normed_mlp = low(norm_rows(resid, gain_mlp))
    gate_pre = low_back(matmul(normed_mlp, w_gate))
    up_pre = low_back(matmul(normed_mlp, w_up))
    hidden = low(jax.nn.silu(gate_pre) * up_pre)
    return resid + matmul(hidden, w_down)

def reference(tokens, segments, positions, attn_gain, mlp_gain, w_query, w_key, w_value, w_output, w_gate, w_up, w_down, cotangent):
    primals = tuple((array_in.astype(jnp.float32) for array_in in (tokens, attn_gain, mlp_gain, w_query, w_key, w_value, w_output, w_gate, w_up, w_down)))

    def forward(inputs, gain_attn, gain_mlp, *matrices):

        def seq_step(params, sequence):
            rows, segment, position = sequence
            return (params, layer(rows, segment, position, params))
        final, outputs = lax.scan(jax.checkpoint(seq_step), (gain_attn, gain_mlp) + tuple(matrices), (inputs.reshape(SEQS, LEN, D), segments, positions))
        return outputs.reshape(SEQS * LEN, D)
    result, pullback = jax.vjp(forward, *primals)
    grads = pullback(cotangent.astype(jnp.float32))
    return (result.astype(jnp.bfloat16), grads[0], grads[1], grads[2], grads[3], grads[4], grads[5], grads[6], grads[7], grads[8], grads[9])
```

```python
import jax
import jax.numpy as jnp
from jax import lax
from jax.sharding import PartitionSpec as P

Q_HEADS = 9
KV_HEADS = 3
HEAD_DIM = 64
LEN = 1024
QBLOCK = 512
QW = 576
KVW = 192


EPS = 1e-05
ROPE_BASE = 100000.0
MASKED = -1e30


def tables(position):
    half_dim = HEAD_DIM // 2
    frequency = ROPE_BASE ** (-(2.0 * jnp.arange(half_dim, dtype=jnp.float32)) / HEAD_DIM)
    angles = position.astype(jnp.float32)[:, None] * frequency[None, :]
    angles = jnp.concatenate([angles, angles], axis=1)
    return (jnp.cos(angles), jnp.sin(angles))


def rotate(values, cosine, sine_table):
    half_dim = HEAD_DIM // 2
    turned = jnp.concatenate([-values[..., half_dim:], values[..., :half_dim]], axis=-1)
    return values * cosine[:, None, :] + turned * sine_table[:, None, :]


def rotate_back(grads, cosine, sine_table):
    half_dim = HEAD_DIM // 2
    scaled = grads * sine_table[:, None, :]
    return grads * cosine[:, None, :] + jnp.concatenate(
        [scaled[..., half_dim:], -scaled[..., :half_dim]], axis=-1
    )


def norm_rows(values):
    inverse = lax.rsqrt(jnp.mean(values * values, axis=-1, keepdims=True) + EPS)
    return (values * inverse, inverse)


def norm_back(grad_scaled, scaled, inverse):
    return inverse * (grad_scaled - scaled * jnp.mean(grad_scaled * scaled, axis=-1, keepdims=True))


def block_scores(queries, keys, segment, block_index, kv_head):
    group_size = Q_HEADS // KV_HEADS
    first_row = block_index * QBLOCK
    row_index = first_row + jnp.arange(QBLOCK, dtype=jnp.int32)
    last_col = first_row + QBLOCK
    col_index = jnp.arange(last_col, dtype=jnp.int32)
    seg_block = segment[first_row : first_row + QBLOCK]
    allowed = (col_index[None, :] <= row_index[:, None]) & (segment[None, :last_col] == seg_block[:, None])
    width = group_size * HEAD_DIM
    query_block = queries[
        first_row : first_row + QBLOCK, kv_head * width : (kv_head + 1) * width
    ].reshape(QBLOCK, group_size, HEAD_DIM)
    key_head = keys[:last_col, kv_head * HEAD_DIM : (kv_head + 1) * HEAD_DIM]
    scores = jnp.einsum(
        "qgd,td->gqt", query_block, key_head, preferred_element_type=jnp.float32
    ) * HEAD_DIM ** (-0.5)
    return (query_block, key_head, jnp.where(allowed[None], scores, MASKED))


def attend_forward(sequence):
    queries, keys, values, segment = sequence
    group_size = Q_HEADS // KV_HEADS
    block_rows, top_list, total_list = ([], [], [])
    for block_index in range(LEN // QBLOCK):
        head_rows, head_tops, head_totals = ([], [], [])
        for kv_head in range(KV_HEADS):
            query_block, key_head, scores = block_scores(
                queries, keys, segment, block_index, kv_head
            )
            top_value = jnp.max(scores, axis=-1, keepdims=True)
            expo = jnp.exp(scores - top_value)
            total = jnp.sum(expo, axis=-1, keepdims=True)
            probability = (expo / total).astype(jnp.bfloat16)
            value_head = values[: (block_index + 1) * QBLOCK, kv_head * HEAD_DIM : (kv_head + 1) * HEAD_DIM]
            attended = jnp.einsum(
                "gqt,td->qgd", probability, value_head, preferred_element_type=jnp.float32
            )
            head_rows.append(attended.reshape(QBLOCK, group_size * HEAD_DIM))
            head_tops.append(top_value)
            head_totals.append(total)
        block_rows.append(jnp.concatenate(head_rows, axis=1))
        top_list.append(jnp.stack(head_tops))
        total_list.append(jnp.stack(head_totals))
    mixture = jnp.concatenate(block_rows, axis=0).astype(jnp.bfloat16)
    return (mixture, jnp.stack(top_list), jnp.stack(total_list))


def attend_backward(sequence):
    queries, keys, values, segment, tops, totals, grad_mixture = sequence
    group_size = Q_HEADS // KV_HEADS
    scale = HEAD_DIM ** (-0.5)
    width = group_size * HEAD_DIM
    grad_key_heads = [None] * KV_HEADS
    grad_value_heads = [None] * KV_HEADS
    block_rows = []
    for block_index in range(LEN // QBLOCK):
        first_row = block_index * QBLOCK
        head_rows = []
        for kv_head in range(KV_HEADS):
            query_block, key_head, scores = block_scores(
                queries, keys, segment, block_index, kv_head
            )
            expo = jnp.exp(scores - tops[block_index, kv_head])
            prob_full = expo / totals[block_index, kv_head]
            probability = prob_full.astype(jnp.bfloat16)
            value_head = values[: (block_index + 1) * QBLOCK, kv_head * HEAD_DIM : (kv_head + 1) * HEAD_DIM]
            grad_block = grad_mixture[
                first_row : first_row + QBLOCK, kv_head * width : (kv_head + 1) * width
            ].reshape(QBLOCK, group_size, HEAD_DIM)
            grad_probs = jnp.einsum(
                "qgd,td->gqt", grad_block, value_head, preferred_element_type=jnp.float32
            )
            grad_value_heads[kv_head] = add_rows(
                grad_value_heads[kv_head],
                jnp.einsum(
                    "gqt,qgd->td", probability, grad_block, preferred_element_type=jnp.float32
                ),
            )
            delta = jnp.sum(prob_full * grad_probs, axis=-1, keepdims=True)
            grad_scores = (prob_full * (grad_probs - delta)).astype(jnp.bfloat16)
            grad_query_block = (
                jnp.einsum("gqt,td->qgd", grad_scores, key_head, preferred_element_type=jnp.float32)
                * scale
            )
            grad_key_heads[kv_head] = add_rows(
                grad_key_heads[kv_head],
                jnp.einsum(
                    "gqt,qgd->td", grad_scores, query_block, preferred_element_type=jnp.float32
                )
                * scale,
            )
            head_rows.append(grad_query_block.reshape(QBLOCK, width))
        block_rows.append(jnp.concatenate(head_rows, axis=1))
    grad_queries = jnp.concatenate(block_rows, axis=0)
    return (
        grad_queries,
        jnp.concatenate(grad_key_heads, axis=1),
        jnp.concatenate(grad_value_heads, axis=1),
    )


def add_rows(longest, shorter):
    if longest is None:
        return shorter
    rows = longest.shape[0]
    return jnp.concatenate([shorter[:rows] + longest, shorter[rows:]], axis=0)


def pack_columns(parts):
    width = sum(part.shape[-1] for part in parts)
    packed = jnp.concatenate(parts, axis=-1)
    return jnp.pad(packed, [(0, 0)] * (packed.ndim - 1) + [(0, -width % 128)])


def gather_pack(packed):
    rows = lax.all_gather(packed, "fsdp", axis=0, tiled=True)
    return lax.all_gather(rows, "dp", axis=0, tiled=False)


def split_columns(packed, widths):
    parts, start = ([], 0)
    for width in widths:
        parts.append(packed[..., start : start + width])
        start += width
    return parts


def split_full(packed, widths):
    pieces = packed.shape[0]
    return [
        part[0]
        if width == 1
        else jnp.concatenate([part[piece] for piece in range(pieces)], axis=1)
        for part, width in zip(split_columns(packed, widths), widths)
    ]


def reduce_pack(matrices, vectors, model_part):
    pieces = lax.axis_size("dp")
    blocks = []
    for piece in range(pieces):
        columns = []
        for matrix in matrices:
            width = matrix.shape[1] // pieces
            columns.append(matrix[:, piece * width : (piece + 1) * width])
        blocks.append(pack_columns(columns + list(vectors)).astype(jnp.bfloat16))
    sent = jnp.stack(blocks)
    got = lax.all_to_all(sent, "dp", 0, 0, tiled=True)
    half = jnp.sum(got.astype(jnp.float32), axis=0)
    shares = half.reshape(half.shape[0] // model_part, model_part, half.shape[1])
    shares = lax.all_to_all(shares.astype(jnp.bfloat16), "fsdp", 0, 0, tiled=True)
    return jnp.sum(shares.astype(jnp.float32), axis=0)


def on_device(
    tokens,
    segments,
    positions,
    attn_gain,
    mlp_gain,
    w_query,
    w_key,
    w_value,
    w_output,
    w_gate,
    w_up,
    w_down,
    cotangent,
):
    model_part = attn_gain.shape[0]
    attn_widths = (w_query.shape[1], w_output.shape[0], w_key.shape[1], w_value.shape[1], 1, 1)
    mlp_widths = (w_gate.shape[1], w_up.shape[1], w_down.shape[0])
    attn_pack = pack_columns(
        (w_query, w_output.T, w_key, w_value, attn_gain[:, None], mlp_gain[:, None])
    )
    mlp_pack = pack_columns((w_gate, w_up, w_down.T))
    attn_all = gather_pack(attn_pack)
    mlp_all = gather_pack(mlp_pack)
    full_query, full_output, full_key, full_value, gains_attn, gains_mlp = split_full(
        attn_all, attn_widths
    )
    full_gate, full_up, full_down = split_full(mlp_all, mlp_widths)
    weights = (
        gains_attn[:, 0],
        gains_mlp[:, 0],
        full_query,
        full_key,
        full_value,
        full_output,
        full_gate,
        full_up,
        full_down,
    )
    row_count = tokens.shape[0]
    seq_count = segments.shape[0]
    gain_attn = weights[0].astype(jnp.float32)
    gain_mlp = weights[1].astype(jnp.float32)
    inputs = tokens.astype(jnp.float32)
    cosine, sine_table = tables(positions.reshape(row_count))
    scaled_attn, inverse_attn = norm_rows(inputs)
    normed_attn = (scaled_attn * gain_attn).astype(jnp.bfloat16)
    query_raw = jnp.dot(normed_attn, weights[2], preferred_element_type=jnp.float32)
    key_raw = jnp.dot(normed_attn, weights[3], preferred_element_type=jnp.float32)
    value_raw = jnp.dot(normed_attn, weights[4], preferred_element_type=jnp.float32)
    queries = (
        rotate(query_raw.reshape(row_count, Q_HEADS, HEAD_DIM), cosine, sine_table)
        .reshape(row_count, QW)
        .astype(jnp.bfloat16)
    )
    keys = (
        rotate(key_raw.reshape(row_count, KV_HEADS, HEAD_DIM), cosine, sine_table)
        .reshape(row_count, KVW)
        .astype(jnp.bfloat16)
    )
    values = value_raw.astype(jnp.bfloat16)
    seq_queries = queries.reshape(seq_count, LEN, QW)
    seq_keys = keys.reshape(seq_count, LEN, KVW)
    seq_values = values.reshape(seq_count, LEN, KVW)
    mixture, tops, totals = lax.map(attend_forward, (seq_queries, seq_keys, seq_values, segments))
    mixture = mixture.reshape(row_count, QW)
    resid = inputs + jnp.einsum("rq,dq->rd", mixture, weights[5], preferred_element_type=jnp.float32)
    scaled_mlp, inverse_mlp = norm_rows(resid)
    normed_mlp = (scaled_mlp * gain_mlp).astype(jnp.bfloat16)
    gate_pre = jnp.dot(normed_mlp, weights[6], preferred_element_type=jnp.float32)
    up_pre = jnp.dot(normed_mlp, weights[7], preferred_element_type=jnp.float32)
    hidden = (jax.nn.silu(gate_pre) * up_pre).astype(jnp.bfloat16)
    output = (resid + jnp.einsum("rf,df->rd", hidden, weights[8], preferred_element_type=jnp.float32)).astype(
        jnp.bfloat16
    )
    back_weights = weights
    grad_down = jnp.einsum("rd,rf->df", cotangent, hidden, preferred_element_type=jnp.float32)
    grad_hidden = jnp.einsum(
        "rd,df->rf", cotangent, back_weights[8], preferred_element_type=jnp.float32
    )
    sigmoid = jax.nn.sigmoid(gate_pre)
    grad_gate_pre = (grad_hidden * up_pre * sigmoid * (1.0 + gate_pre * (1.0 - sigmoid))).astype(
        jnp.bfloat16
    )
    grad_up_pre = (grad_hidden * (gate_pre * sigmoid)).astype(jnp.bfloat16)
    grad_gate = jnp.einsum(
        "rd,rf->df", normed_mlp, grad_gate_pre, preferred_element_type=jnp.float32
    )
    grad_up = jnp.einsum("rd,rf->df", normed_mlp, grad_up_pre, preferred_element_type=jnp.float32)
    grad_normed_mlp = jnp.einsum(
        "rf,df->rd", grad_gate_pre, back_weights[6], preferred_element_type=jnp.float32
    )
    grad_normed_mlp = grad_normed_mlp + jnp.einsum(
        "rf,df->rd", grad_up_pre, back_weights[7], preferred_element_type=jnp.float32
    )
    grad_mlp_gain = jnp.sum(grad_normed_mlp * scaled_mlp, axis=0)
    grad_resid = cotangent.astype(jnp.float32) + norm_back(
        grad_normed_mlp * back_weights[1].astype(jnp.float32), scaled_mlp, inverse_mlp
    )
    grad_branch = grad_resid.astype(jnp.bfloat16)
    grad_output = jnp.einsum("rd,rq->dq", grad_branch, mixture, preferred_element_type=jnp.float32)
    grad_mixture = jnp.einsum(
        "rd,dq->rq", grad_branch, back_weights[5], preferred_element_type=jnp.float32
    ).astype(jnp.bfloat16)
    grad_queries, grad_keys, grad_values = lax.map(
        attend_backward,
        (
            seq_queries,
            seq_keys,
            seq_values,
            segments,
            tops,
            totals,
            grad_mixture.reshape(seq_count, LEN, QW),
        ),
    )
    grad_query_raw = (
        rotate_back(grad_queries.reshape(row_count, Q_HEADS, HEAD_DIM), cosine, sine_table)
        .reshape(row_count, QW)
        .astype(jnp.bfloat16)
    )
    grad_key_raw = (
        rotate_back(grad_keys.reshape(row_count, KV_HEADS, HEAD_DIM), cosine, sine_table)
        .reshape(row_count, KVW)
        .astype(jnp.bfloat16)
    )
    grad_value_raw = grad_values.reshape(row_count, KVW).astype(jnp.bfloat16)
    grad_query = jnp.einsum(
        "rd,rq->dq", normed_attn, grad_query_raw, preferred_element_type=jnp.float32
    )
    grad_key = jnp.einsum(
        "rd,rq->dq", normed_attn, grad_key_raw, preferred_element_type=jnp.float32
    )
    grad_value = jnp.einsum(
        "rd,rq->dq", normed_attn, grad_value_raw, preferred_element_type=jnp.float32
    )
    grad_normed_attn = jnp.einsum(
        "rq,dq->rd", grad_query_raw, back_weights[2], preferred_element_type=jnp.float32
    )
    grad_normed_attn = grad_normed_attn + jnp.einsum(
        "rq,dq->rd", grad_key_raw, back_weights[3], preferred_element_type=jnp.float32
    )
    grad_normed_attn = grad_normed_attn + jnp.einsum(
        "rq,dq->rd", grad_value_raw, back_weights[4], preferred_element_type=jnp.float32
    )
    grad_attn_gain = jnp.sum(grad_normed_attn * scaled_attn, axis=0)
    grad_tokens = grad_resid + norm_back(
        grad_normed_attn * back_weights[0].astype(jnp.float32), scaled_attn, inverse_attn
    )
    mlp_sum = reduce_pack((grad_gate, grad_up, grad_down), (), model_part)
    attn_sum = reduce_pack(
        (grad_query, grad_output, grad_key, grad_value),
        (grad_attn_gain[:, None], grad_mlp_gain[:, None]),
        model_part,
    )
    own_gate, own_up, own_down = split_columns(mlp_sum, mlp_widths)
    own_query, own_output, own_key, own_value, own_attn_gain, own_mlp_gain = split_columns(
        attn_sum, attn_widths
    )
    return (
        output,
        grad_tokens,
        own_attn_gain[:, 0],
        own_mlp_gain[:, 0],
        own_query,
        own_key,
        own_value,
        own_output.T,
        own_gate,
        own_up,
        own_down.T,
    )


def solution(mesh):
    in_specs = (
        P(("dp", "fsdp"), None),
        P(("dp", "fsdp"), None),
        P(("dp", "fsdp"), None),
        P("fsdp"),
        P("fsdp"),
        P("fsdp", "dp"),
        P("fsdp", "dp"),
        P("fsdp", "dp"),
        P("dp", "fsdp"),
        P("fsdp", "dp"),
        P("fsdp", "dp"),
        P("dp", "fsdp"),
        P(("dp", "fsdp"), None),
    )
    out_specs = (
        P(("dp", "fsdp"), None),
        P(("dp", "fsdp"), None),
        P("fsdp"),
        P("fsdp"),
        P("fsdp", "dp"),
        P("fsdp", "dp"),
        P("fsdp", "dp"),
        P("dp", "fsdp"),
        P("fsdp", "dp"),
        P("fsdp", "dp"),
        P("dp", "fsdp"),
    )
    return jax.shard_map(
        on_device, mesh=mesh, in_specs=in_specs, out_specs=out_specs, check_vma=False
    )
```

```python
import jax
import jax.numpy as jnp
from jax import lax
from jax.sharding import PartitionSpec as P

Q_HEADS = 9
KV_HEADS = 3
HEAD_DIM = 64
LEN = 1024
QBLOCK = 512
QW = 576
KVW = 192


EPS = 1e-05
ROPE_BASE = 100000.0
MASKED = -1e30


def tables(position):
    half_dim = HEAD_DIM // 2
    frequency = ROPE_BASE ** (-(2.0 * jnp.arange(half_dim, dtype=jnp.float32)) / HEAD_DIM)
    angles = position.astype(jnp.float32)[:, None] * frequency[None, :]
    angles = jnp.concatenate([angles, angles], axis=1)
    return (jnp.cos(angles), jnp.sin(angles))


def rotate(values, cosine, sine_table):
    half_dim = HEAD_DIM // 2
    turned = jnp.concatenate([-values[..., half_dim:], values[..., :half_dim]], axis=-1)
    return values * cosine[:, None, :] + turned * sine_table[:, None, :]


def rotate_back(grads, cosine, sine_table):
    half_dim = HEAD_DIM // 2
    scaled = grads * sine_table[:, None, :]
    return grads * cosine[:, None, :] + jnp.concatenate(
        [scaled[..., half_dim:], -scaled[..., :half_dim]], axis=-1
    )


def norm_rows(values):
    inverse = lax.rsqrt(jnp.mean(values * values, axis=-1, keepdims=True) + EPS)
    return (values * inverse, inverse)


def norm_back(grad_scaled, scaled, inverse):
    return inverse * (grad_scaled - scaled * jnp.mean(grad_scaled * scaled, axis=-1, keepdims=True))


def block_scores(queries, keys, segment, block_index, kv_head):
    group_size = Q_HEADS // KV_HEADS
    first_row = block_index * QBLOCK
    row_index = first_row + jnp.arange(QBLOCK, dtype=jnp.int32)
    last_col = first_row + QBLOCK
    col_index = jnp.arange(last_col, dtype=jnp.int32)
    seg_block = segment[first_row : first_row + QBLOCK]
    allowed = (col_index[None, :] <= row_index[:, None]) & (segment[None, :last_col] == seg_block[:, None])
    width = group_size * HEAD_DIM
    query_block = queries[
        first_row : first_row + QBLOCK, kv_head * width : (kv_head + 1) * width
    ].reshape(QBLOCK, group_size, HEAD_DIM)
    key_head = keys[:last_col, kv_head * HEAD_DIM : (kv_head + 1) * HEAD_DIM]
    scores = jnp.einsum(
        "qgd,td->gqt", query_block, key_head, preferred_element_type=jnp.float32
    ) * HEAD_DIM ** (-0.5)
    return (query_block, key_head, jnp.where(allowed[None], scores, MASKED))


def attend_forward(sequence):
    queries, keys, values, segment = sequence
    group_size = Q_HEADS // KV_HEADS
    block_rows, top_list, total_list = ([], [], [])
    for block_index in range(LEN // QBLOCK):
        head_rows, head_tops, head_totals = ([], [], [])
        for kv_head in range(KV_HEADS):
            query_block, key_head, scores = block_scores(
                queries, keys, segment, block_index, kv_head
            )
            top_value = jnp.max(scores, axis=-1, keepdims=True)
            expo = jnp.exp(scores - top_value)
            total = jnp.sum(expo, axis=-1, keepdims=True)
            probability = (expo / total).astype(jnp.bfloat16)
            value_head = values[: (block_index + 1) * QBLOCK, kv_head * HEAD_DIM : (kv_head + 1) * HEAD_DIM]
            attended = jnp.einsum(
                "gqt,td->qgd", probability, value_head, preferred_element_type=jnp.float32
            )
            head_rows.append(attended.reshape(QBLOCK, group_size * HEAD_DIM))
            head_tops.append(top_value)
            head_totals.append(total)
        block_rows.append(jnp.concatenate(head_rows, axis=1))
        top_list.append(jnp.stack(head_tops))
        total_list.append(jnp.stack(head_totals))
    mixture = jnp.concatenate(block_rows, axis=0).astype(jnp.bfloat16)
    return (mixture, jnp.stack(top_list), jnp.stack(total_list))


def attend_backward(sequence):
    queries, keys, values, segment, tops, totals, grad_mixture = sequence
    group_size = Q_HEADS // KV_HEADS
    scale = HEAD_DIM ** (-0.5)
    width = group_size * HEAD_DIM
    grad_key_heads = [None] * KV_HEADS
    grad_value_heads = [None] * KV_HEADS
    block_rows = []
    for block_index in range(LEN // QBLOCK):
        first_row = block_index * QBLOCK
        head_rows = []
        for kv_head in range(KV_HEADS):
            query_block, key_head, scores = block_scores(
                queries, keys, segment, block_index, kv_head
            )
            expo = jnp.exp(scores - tops[block_index, kv_head])
            prob_full = expo / totals[block_index, kv_head]
            probability = prob_full.astype(jnp.bfloat16)
            value_head = values[: (block_index + 1) * QBLOCK, kv_head * HEAD_DIM : (kv_head + 1) * HEAD_DIM]
            grad_block = grad_mixture[
                first_row : first_row + QBLOCK, kv_head * width : (kv_head + 1) * width
            ].reshape(QBLOCK, group_size, HEAD_DIM)
            grad_probs = jnp.einsum(
                "qgd,td->gqt", grad_block, value_head, preferred_element_type=jnp.float32
            )
            grad_value_heads[kv_head] = add_rows(
                grad_value_heads[kv_head],
                jnp.einsum(
                    "gqt,qgd->td", probability, grad_block, preferred_element_type=jnp.float32
                ),
            )
            delta = jnp.sum(prob_full * grad_probs, axis=-1, keepdims=True)
            grad_scores = (prob_full * (grad_probs - delta)).astype(jnp.bfloat16)
            grad_query_block = (
                jnp.einsum("gqt,td->qgd", grad_scores, key_head, preferred_element_type=jnp.float32)
                * scale
            )
            grad_key_heads[kv_head] = add_rows(
                grad_key_heads[kv_head],
                jnp.einsum(
                    "gqt,qgd->td", grad_scores, query_block, preferred_element_type=jnp.float32
                )
                * scale,
            )
            head_rows.append(grad_query_block.reshape(QBLOCK, width))
        block_rows.append(jnp.concatenate(head_rows, axis=1))
    grad_queries = jnp.concatenate(block_rows, axis=0)
    return (
        grad_queries,
        jnp.concatenate(grad_key_heads, axis=1),
        jnp.concatenate(grad_value_heads, axis=1),
    )


def add_rows(longest, shorter):
    if longest is None:
        return shorter
    rows = longest.shape[0]
    return jnp.concatenate([shorter[:rows] + longest, shorter[rows:]], axis=0)


def pack_columns(parts):
    width = sum(part.shape[-1] for part in parts)
    packed = jnp.concatenate(parts, axis=-1)
    return jnp.pad(packed, [(0, 0)] * (packed.ndim - 1) + [(0, -width % 128)])


def gather_pack(packed):
    rows = lax.all_gather(packed, "fsdp", axis=0, tiled=True)
    return lax.all_gather(rows, "dp", axis=0, tiled=False)


def split_columns(packed, widths):
    parts, start = ([], 0)
    for width in widths:
        parts.append(packed[..., start : start + width])
        start += width
    return parts


def split_full(packed, widths):
    pieces = packed.shape[0]
    return [
        part[0]
        if width == 1
        else jnp.concatenate([part[piece] for piece in range(pieces)], axis=1)
        for part, width in zip(split_columns(packed, widths), widths)
    ]


def pack_grads(matrices, vectors=()):
    pieces = lax.axis_size("dp")
    blocks = []
    for piece in range(pieces):
        columns = []
        for matrix in matrices:
            width = matrix.shape[1] // pieces
            columns.append(matrix[:, piece * width : (piece + 1) * width])
        blocks.append(pack_columns(columns + list(vectors)).astype(jnp.bfloat16))
    return jnp.stack(blocks)


def exchange(sent):
    return lax.all_to_all(sent, "dp", 0, 0, tiled=True)


def reduce_pack(got, model_part):
    half = jnp.sum(got.astype(jnp.float32), axis=0)
    shares = half.reshape(half.shape[0] // model_part, model_part, half.shape[1])
    shares = lax.all_to_all(shares.astype(jnp.bfloat16), "fsdp", 0, 0, tiled=True)
    return jnp.sum(shares.astype(jnp.float32), axis=0)


def on_device(
    tokens,
    segments,
    positions,
    attn_gain,
    mlp_gain,
    w_query,
    w_key,
    w_value,
    w_output,
    w_gate,
    w_up,
    w_down,
    cotangent,
):
    model_part = attn_gain.shape[0]
    attn_widths = (w_query.shape[1], w_output.shape[0], w_key.shape[1], w_value.shape[1], 1, 1)
    mlp_widths = (w_gate.shape[1], w_up.shape[1], w_down.shape[0])
    attn_pack = pack_columns(
        (w_query, w_output.T, w_key, w_value, attn_gain[:, None], mlp_gain[:, None])
    )
    mlp_pack = pack_columns((w_gate, w_up, w_down.T))
    attn_all = gather_pack(attn_pack)
    mlp_pack, attn_all = lax.optimization_barrier((mlp_pack, attn_all))
    mlp_all = gather_pack(mlp_pack)
    full_query, full_output, full_key, full_value, gains_attn, gains_mlp = split_full(
        attn_all, attn_widths
    )
    full_gate, full_up, full_down = split_full(mlp_all, mlp_widths)
    weights = (
        gains_attn[:, 0],
        gains_mlp[:, 0],
        full_query,
        full_key,
        full_value,
        full_output,
        full_gate,
        full_up,
        full_down,
    )
    row_count = tokens.shape[0]
    seq_count = segments.shape[0]
    gain_attn = weights[0].astype(jnp.float32)
    gain_mlp = weights[1].astype(jnp.float32)
    inputs = tokens.astype(jnp.float32)
    cosine, sine_table = tables(positions.reshape(row_count))
    scaled_attn, inverse_attn = norm_rows(inputs)
    normed_attn = (scaled_attn * gain_attn).astype(jnp.bfloat16)
    query_raw = jnp.dot(normed_attn, weights[2], preferred_element_type=jnp.float32)
    key_raw = jnp.dot(normed_attn, weights[3], preferred_element_type=jnp.float32)
    value_raw = jnp.dot(normed_attn, weights[4], preferred_element_type=jnp.float32)
    queries = (
        rotate(query_raw.reshape(row_count, Q_HEADS, HEAD_DIM), cosine, sine_table)
        .reshape(row_count, QW)
        .astype(jnp.bfloat16)
    )
    keys = (
        rotate(key_raw.reshape(row_count, KV_HEADS, HEAD_DIM), cosine, sine_table)
        .reshape(row_count, KVW)
        .astype(jnp.bfloat16)
    )
    values = value_raw.astype(jnp.bfloat16)
    seq_queries = queries.reshape(seq_count, LEN, QW)
    seq_keys = keys.reshape(seq_count, LEN, KVW)
    seq_values = values.reshape(seq_count, LEN, KVW)
    mixture, tops, totals = lax.map(attend_forward, (seq_queries, seq_keys, seq_values, segments))
    mixture = mixture.reshape(row_count, QW)
    resid = inputs + jnp.einsum("rq,dq->rd", mixture, weights[5], preferred_element_type=jnp.float32)
    scaled_mlp, inverse_mlp = norm_rows(resid)
    normed_mlp = (scaled_mlp * gain_mlp).astype(jnp.bfloat16)
    gate_pre = jnp.dot(normed_mlp, weights[6], preferred_element_type=jnp.float32)
    up_pre = jnp.dot(normed_mlp, weights[7], preferred_element_type=jnp.float32)
    hidden = (jax.nn.silu(gate_pre) * up_pre).astype(jnp.bfloat16)
    output = (resid + jnp.einsum("rf,df->rd", hidden, weights[8], preferred_element_type=jnp.float32)).astype(
        jnp.bfloat16
    )
    back_weights = weights
    grad_down = jnp.einsum("rd,rf->df", cotangent, hidden, preferred_element_type=jnp.float32)
    grad_hidden = jnp.einsum(
        "rd,df->rf", cotangent, back_weights[8], preferred_element_type=jnp.float32
    )
    sigmoid = jax.nn.sigmoid(gate_pre)
    grad_gate_pre = (grad_hidden * up_pre * sigmoid * (1.0 + gate_pre * (1.0 - sigmoid))).astype(
        jnp.bfloat16
    )
    grad_up_pre = (grad_hidden * (gate_pre * sigmoid)).astype(jnp.bfloat16)
    grad_gate = jnp.einsum(
        "rd,rf->df", normed_mlp, grad_gate_pre, preferred_element_type=jnp.float32
    )
    grad_up = jnp.einsum("rd,rf->df", normed_mlp, grad_up_pre, preferred_element_type=jnp.float32)
    grad_normed_mlp = jnp.einsum(
        "rf,df->rd", grad_gate_pre, back_weights[6], preferred_element_type=jnp.float32
    )
    grad_normed_mlp = grad_normed_mlp + jnp.einsum(
        "rf,df->rd", grad_up_pre, back_weights[7], preferred_element_type=jnp.float32
    )
    grad_mlp_gain = jnp.sum(grad_normed_mlp * scaled_mlp, axis=0)
    grad_resid = cotangent.astype(jnp.float32) + norm_back(
        grad_normed_mlp * back_weights[1].astype(jnp.float32), scaled_mlp, inverse_mlp
    )
    mlp_sent = pack_grads((grad_gate, grad_up, grad_down))
    grad_resid, mlp_sent = lax.optimization_barrier((grad_resid, mlp_sent))
    mlp_got = exchange(mlp_sent)
    grad_branch = grad_resid.astype(jnp.bfloat16)
    grad_output = jnp.einsum("rd,rq->dq", grad_branch, mixture, preferred_element_type=jnp.float32)
    grad_mixture = jnp.einsum(
        "rd,dq->rq", grad_branch, back_weights[5], preferred_element_type=jnp.float32
    ).astype(jnp.bfloat16)
    grad_queries, grad_keys, grad_values = lax.map(
        attend_backward,
        (
            seq_queries,
            seq_keys,
            seq_values,
            segments,
            tops,
            totals,
            grad_mixture.reshape(seq_count, LEN, QW),
        ),
    )
    grad_query_raw = (
        rotate_back(grad_queries.reshape(row_count, Q_HEADS, HEAD_DIM), cosine, sine_table)
        .reshape(row_count, QW)
        .astype(jnp.bfloat16)
    )
    grad_key_raw = (
        rotate_back(grad_keys.reshape(row_count, KV_HEADS, HEAD_DIM), cosine, sine_table)
        .reshape(row_count, KVW)
        .astype(jnp.bfloat16)
    )
    grad_value_raw = grad_values.reshape(row_count, KVW).astype(jnp.bfloat16)
    grad_query_raw, mlp_got = lax.optimization_barrier((grad_query_raw, mlp_got))
    mlp_sum = reduce_pack(mlp_got, model_part)
    grad_query = jnp.einsum(
        "rd,rq->dq", normed_attn, grad_query_raw, preferred_element_type=jnp.float32
    )
    grad_key = jnp.einsum(
        "rd,rq->dq", normed_attn, grad_key_raw, preferred_element_type=jnp.float32
    )
    grad_value = jnp.einsum(
        "rd,rq->dq", normed_attn, grad_value_raw, preferred_element_type=jnp.float32
    )
    grad_normed_attn = jnp.einsum(
        "rq,dq->rd", grad_query_raw, back_weights[2], preferred_element_type=jnp.float32
    )
    grad_normed_attn = grad_normed_attn + jnp.einsum(
        "rq,dq->rd", grad_key_raw, back_weights[3], preferred_element_type=jnp.float32
    )
    grad_normed_attn = grad_normed_attn + jnp.einsum(
        "rq,dq->rd", grad_value_raw, back_weights[4], preferred_element_type=jnp.float32
    )
    grad_attn_gain = jnp.sum(grad_normed_attn * scaled_attn, axis=0)
    grad_tokens = grad_resid + norm_back(
        grad_normed_attn * back_weights[0].astype(jnp.float32), scaled_attn, inverse_attn
    )
    attn_sent = pack_grads(
        (grad_query, grad_output, grad_key, grad_value),
        (grad_attn_gain[:, None], grad_mlp_gain[:, None]),
    )
    attn_sum = reduce_pack(exchange(attn_sent), model_part)
    own_gate, own_up, own_down = split_columns(mlp_sum, mlp_widths)
    own_query, own_output, own_key, own_value, own_attn_gain, own_mlp_gain = split_columns(
        attn_sum, attn_widths
    )
    return (
        output,
        grad_tokens,
        own_attn_gain[:, 0],
        own_mlp_gain[:, 0],
        own_query,
        own_key,
        own_value,
        own_output.T,
        own_gate,
        own_up,
        own_down.T,
    )


def solution(mesh):
    in_specs = (
        P(("dp", "fsdp"), None),
        P(("dp", "fsdp"), None),
        P(("dp", "fsdp"), None),
        P("fsdp"),
        P("fsdp"),
        P("fsdp", "dp"),
        P("fsdp", "dp"),
        P("fsdp", "dp"),
        P("dp", "fsdp"),
        P("fsdp", "dp"),
        P("fsdp", "dp"),
        P("dp", "fsdp"),
        P(("dp", "fsdp"), None),
    )
    out_specs = (
        P(("dp", "fsdp"), None),
        P(("dp", "fsdp"), None),
        P("fsdp"),
        P("fsdp"),
        P("fsdp", "dp"),
        P("fsdp", "dp"),
        P("fsdp", "dp"),
        P("dp", "fsdp"),
        P("fsdp", "dp"),
        P("fsdp", "dp"),
        P("dp", "fsdp"),
    )
    return jax.shard_map(
        on_device, mesh=mesh, in_specs=in_specs, out_specs=out_specs, check_vma=False
    )
```
